256 devices in a mesh: tm: 64 (over z, y, core), head: 4 (over x).
Axes of the slice: x: 4, y: 4, z: 8, core: 2. Of those that a mesh axis runs over, the one named last changes fastest.
Arguments:
- tokens: bfloat16 [65536, 2048], P(('tm', 'head')), may hold values from -6 to 6
- frame_counts: int32 [512], P('tm'), may hold values from 1 to 128, 32768 in all
- decay_log: float32 [16, 65536], P('head', 'tm'), may hold values from -3 to 0
- norm_gain: float32 [2048], replicated, may hold values from 0.1 to 1.9
- w_qkv: bfloat16 [2048, 3, 2048], P(None, None, 'head'), may hold values from -0.125 to 0.125
- head_gain: float32 [2048], P('head'), may hold values from 0.1 to 1.9
- w_out: bfloat16 [2048, 2048], P('head'), may hold values from -0.125 to 0.125
Outputs:
- mixed: bfloat16 [65536, 2048], P(('tm', 'head'))
The draws below stay inside these ranges and needn't reach their ends.
Inputs may be any that keep to these rules, and one draw needn't show every extreme that they name: `frame_counts`: the counts of all 512 frames add up to 32768.
All inputs are finite; a program needn't handle non-finite values. No bound on the sum of `frame_counts` on one device may be relied on, other than what follows from the above.
Results may differ from the reference program's by a relative error of at most 0.0074.
Values may be sent and summed in bfloat16 or wider, within the bound.
A program may use at most 128 MiB of HBM per device.

```python
import math
import jax
import jax.numpy as jnp
import numpy as np
from jax import lax

D = 2048
HEADS = 16
HD = 128
FCAP = 128
INNER = 2048
CAP = 1024
FRAMES = 512
SLOTS = 65536
N_TM = 64


def draw_decay_log(key, part):
    keys = jax.random.split(jax.random.fold_in(key, 17), 7)
    fast_count = 4
    token_factor = jnp.exp(jax.random.uniform(keys[0], (HEADS, SLOTS), jnp.float32, jnp.log(0.5), jnp.log(2.0)))
    rate_slow = jnp.exp(jax.random.uniform(keys[3], (HEADS,), jnp.float32, jnp.log(0.3), jnp.log(0.6))) / CAP
    fast = jax.random.randint(keys[1], (HEADS,), 0, 8) < fast_count
    rate_fast = jnp.exp(jax.random.uniform(keys[2], (HEADS,), jnp.float32, jnp.log(1.0 / 50.0), jnp.log(1.0 / 30.0)))
    rate = jnp.where(fast, rate_fast, rate_slow)
    block_factor = jnp.exp(jax.random.uniform(keys[4], (HEADS, N_TM), jnp.float32, jnp.log(0.5), jnp.log(2.0)))
    block_factor = jnp.broadcast_to(block_factor[:, :, None], (HEADS, N_TM, CAP)).reshape(HEADS, SLOTS)
    start_index_shift = -rate[:, None] * token_factor * block_factor
    patch_locations = jax.random.randint(keys[5], (3,), 0, SLOTS)
    forgetting_rate = jax.random.uniform(keys[6], (3,), jnp.float32, jnp.log(0.5), jnp.log(0.8))
    padded_entry_index = jnp.arange(SLOTS, dtype=jnp.int32)
    segment_span = jnp.sum(jnp.where(padded_entry_index[None, :] == patch_locations[:, None], forgetting_rate[:, None], 0.0), axis=0)
    return (start_index_shift + segment_span[None, :]).astype(jnp.float32)


def levels(key, shape, shards, low, top_value):
    gain, own = 1.0, jax.random.fold_in(key, 6)
    for dim, blocks in shards:
        draws = jnp.exp(jax.random.uniform(jax.random.fold_in(own, dim), (blocks,), jnp.float32, low / len(shards), top_value / len(shards)))
        gain = gain * jnp.repeat(draws, shape[dim] // blocks).reshape([-1 if axis == dim else 1 for axis in range(len(shape))])
    return gain


def split_up(amount, total, most, slope):
    weights = [(1 << 20) // math.isqrt(grade ** slope) + 1 for grade in range(2, amount + 1)]
    spare, given = total - most - (amount - 1), [1] * (amount - 1)
    while spare > 0:
        movable = [i for i in range(amount - 1) if given[i] < most]
        pool, budget = sum([weights[i] for i in movable]), spare
        for i in movable:
            addition = min(most - given[i], max(1, budget * weights[i] // pool), spare)
            given[i] = given[i] + addition
            spare = spare - addition
    return np.array([most] + given)


def uneven(own_key, count, total, reach, skew):
    if count == 2:
        one = jax.random.randint(own_key, (), max(1, total - reach), min(reach, total - 1) + 1)
        return jnp.stack([one, total - one])
    tallies = jnp.asarray(split_up(count, total, reach, skew), jnp.int32)
    pairs = (count - 1) // 2
    donor, receiver = tallies[1:1 + 2 * pairs:2], tallies[2:2 + 2 * pairs:2]
    margin = jnp.minimum(donor - 1, reach - receiver)
    passed = jax.random.randint(jax.random.fold_in(own_key, 1), (pairs,), 0, 1 << 20) % (margin + 1)
    tallies = tallies.at[1:1 + 2 * pairs:2].set(donor - passed).at[2:2 + 2 * pairs:2].set(receiver + passed)
    return tallies[jax.random.permutation(jax.random.fold_in(own_key, 2), count)]


def noise(stream_key, extent, scale, most, pieces=(), held_as=jnp.bfloat16):
    array = jax.random.normal(stream_key, extent, jnp.float32) * scale
    if len(pieces) > 0:
        array = levels(stream_key, extent, pieces, -0.22, 0.18) * array
    return jnp.clip(array, min=-most, max=most).astype(held_as)


def setup_inputs(seed: int = 0) -> dict:
    seeds = jax.random.split(jax.random.key(seed), 8)
    return {
        "tokens": noise(seeds[0], (SLOTS, D), 1.0, 6.0, ((0, 256),)),
        "frame_counts": uneven(seeds[1], FRAMES, FRAMES * FCAP // 2, FCAP, 2).astype(jnp.int32),
        "decay_log": draw_decay_log(jax.random.fold_in(seeds[7], 71), 0),
        "norm_gain": jnp.clip(1.0 + 0.18 * jax.random.normal(seeds[3], (D,), jnp.float32), 0.1, 1.9),
        "w_qkv": noise(seeds[4], (D, 3, INNER), D ** -0.5, 0.125, ((2, 4),)),
        "head_gain": jnp.clip(1.0 + 0.18 * jax.random.normal(seeds[5], (INNER,), jnp.float32), 0.1, 1.9),
        "w_out": noise(seeds[6], (INNER, D), (HEADS * HD) ** -0.5, 0.125, ((0, 4),)),
    }


def live_rows(counts):
    slot = jnp.arange(FCAP, dtype=jnp.int32)
    return (slot[None, :] < counts[:, None]).reshape(counts.shape[0] * FCAP).astype(jnp.float32)

def rounded(values):
    return lax.optimization_barrier(values.astype(jnp.bfloat16)).astype(jnp.float32)

def reference(tokens, frame_counts, decay_log, norm_gain, w_qkv, head_gain, w_out):
    live = live_rows(frame_counts)
    values = tokens.astype(jnp.float32)
    scale = lax.rsqrt(lax.optimization_barrier(jnp.mean(values * values, axis=1, keepdims=True)) + 1e-05)
    normed = (values * scale * norm_gain).astype(jnp.bfloat16)
    packed = jnp.dot(normed, w_qkv.reshape(D, 3 * INNER), preferred_element_type=jnp.float32).astype(jnp.bfloat16)
    packed = packed.reshape(SLOTS, 3, HEADS, HD)
    query = packed[:, 0].reshape(N_TM, CAP, HEADS, HD)
    keys = (packed[:, 1] * live[:, None, None]).astype(jnp.bfloat16).reshape(N_TM, CAP, HEADS, HD)
    value = packed[:, 2].reshape(N_TM, CAP, HEADS, HD)
    logs = (decay_log * live[None, :]).reshape(HEADS, N_TM, CAP).transpose(1, 0, 2)
    order = jnp.arange(CAP, dtype=jnp.int32)
    causal = order[:, None] >= order[None, :]

    def step(state, block):
        q_blk, k_blk, v_blk, g_blk = block
        qf = q_blk.astype(jnp.float32)
        kf = k_blk.astype(jnp.float32)
        vf = v_blk.astype(jnp.float32)
        running = jnp.cumsum(g_blk, axis=1)
        scores = jnp.einsum('rhe,she->hrs', qf, kf)
        gap = jnp.where(causal[None], running[:, :, None] - running[:, None, :], 0.0)
        weights = rounded(jnp.where(causal[None], scores * jnp.exp(gap), 0.0))
        inside = jnp.einsum('hrs,she->rhe', weights, vf)
        total = running[:, -1]
        tail = jnp.exp(total[:, None] - running)
        scaled = rounded(kf * tail.T[:, :, None])
        local_state = jnp.einsum('she,shf->hef', scaled, vf)
        carried = jnp.einsum('rhe,hef->rhf', qf, rounded(state)) * jnp.exp(running).T[:, :, None]
        new_state = jnp.exp(total)[:, None, None] * state + local_state
        return (new_state, inside + carried)
    start = jnp.zeros((HEADS, HD, HD), jnp.float32)
    _, attended = lax.scan(step, start, (query, keys, value, logs))
    attended = attended.reshape(SLOTS, HEADS, HD)
    attention_gain_per_channel = lax.rsqrt(lax.optimization_barrier(jnp.mean(attended * attended, axis=2, keepdims=True)) + 1e-05)
    heads_out = (attended * attention_gain_per_channel * head_gain.reshape(HEADS, HD)).astype(jnp.bfloat16).reshape(SLOTS, INNER)
    summed = jnp.dot(heads_out, w_out, preferred_element_type=jnp.float32)
    return ((values + summed) * live[:, None]).astype(jnp.bfloat16)
```

```python
import functools

import jax
import jax.numpy as jnp
from jax import lax
from jax.experimental import pallas as pl
from jax.experimental.pallas import tpu as pltpu
from jax.sharding import PartitionSpec as P

MESH = pl.DeviceIdType.MESH
F32 = jnp.float32
BF16 = jnp.bfloat16

FCAP = 128
HD = 128
NX = 4
NP = 8
TM, HEAD = "tm", "head"


def _dot(a, b):
    return jnp.dot(a, b, preferred_element_type=F32)


def _dot_nt(a, b):
    return lax.dot_general(a, b, (((1,), (1,)), ((), ())), preferred_element_type=F32)


def _dot_tn(a, b):
    return lax.dot_general(a, b, (((0,), (0,)), ((), ())), preferred_element_type=F32)


def kernel(
    nz, counts, tok, decay, ngain, hgain, w3, wo, out,
    xall, nrm, wq, qkv, ins, wg, acc, crow, ccb, liveb, dec, ngv, hgv,
    st_acc, st_send, st_recv, inner, pl_send, pl_recv, tot_send, tot_recv,
    pt_send, pt_recv, pr_send, prior, ho_s, ho_r, relay, lsem, ssem, rsem,
):
    rows = xall.shape[1]
    half = rows // 2
    cap = NX * rows
    width = xall.shape[2]
    inn = hgv.shape[1]
    nh = inn // HD
    piece = st_send.shape[1]
    wrow = inn // (nz * NP // 2)
    wcol = width // 2

    tm = lax.axis_index(TM)
    x = lax.axis_index(HEAD)
    z = tm // NP
    p = lax.rem(tm, NP)
    y = p // 2
    core = lax.rem(p, 2)
    xr, xo, xl = lax.rem(x + 1, NX), lax.rem(x + 2, NX), lax.rem(x + 3, NX)

    def plane(d):
        return lax.rem(p + d, NP)

    def zed(d):
        return lax.rem(z + d + nz, nz)

    loads = [
        pltpu.make_async_copy(decay, dec, lsem.at[0]),
        pltpu.make_async_copy(tok, xall.at[x], lsem.at[1]),
        pltpu.make_async_copy(ngain, ngv, lsem.at[2]),
        pltpu.make_async_copy(hgain, hgv, lsem.at[3]),
        pltpu.make_async_copy(w3, wq, lsem.at[4]),
        pltpu.make_async_copy(wo, wg.at[0], lsem.at[5]),
    ]
    for c in loads:
        c.start()

    barrier = pltpu.get_barrier_semaphore()
    for d in range(1, NX):
        pl.semaphore_signal(barrier, inc=1, device_id=(tm, lax.rem(x + d, NX)), device_id_type=MESH)
    for d in range(1, NP):
        pl.semaphore_signal(barrier, inc=1, device_id=(z * NP + plane(d), x), device_id_type=MESH)
    for d in range(1, nz):
        pl.semaphore_signal(barrier, inc=1, device_id=(zed(d) * NP + p, x), device_id_type=MESH)
    pl.semaphore_wait(barrier, NX - 1 + NP - 1 + nz - 1)

    counter = [0]
    started, by_core, slots = [], ([], []), {}

    def remote(src, dst, dev, who=None):
        i = counter[0]
        counter[0] += 1
        c = pltpu.make_async_remote_copy(
            src_ref=src, dst_ref=dst, send_sem=ssem.at[i], recv_sem=rsem.at[i],
            device_id=dev, device_id_type=MESH,
        )
        (started if who is None else by_core[who]).append(c)
        slots[id(c)] = (i, dev)
        return c

    def landing(c, dst):
        i, dev = slots[id(c)]
        return pltpu.make_async_remote_copy(
            src_ref=dst, dst_ref=dst, send_sem=ssem.at[i], recv_sem=rsem.at[i],
            device_id=dev, device_id_type=MESH,
        )

    right, left = (tm, xr), (tm, xl)
    top, bot = pl.ds(0, half), pl.ds(half, half)

    ny = NP // 2
    wcols = pl.ds(pl.multiple_of(core * wcol, wcol), wcol)
    wr0 = pl.multiple_of(((1 - core) * (z * ny + y) + core * (y * nz + z)) * wrow, wrow)
    wx = []
    for d in range(1, NX):
        c = remote(
            wo.at[pl.ds(wr0, wrow), wcols], wg.at[NX - d, pl.ds(wr0, wrow), wcols],
            (tm, lax.rem(x + d, NX)),
        )
        c.start()
        wx.append(landing(c, wg.at[NX - d, pl.ds(wr0, wrow), wcols]))

    q0, q1, q2, q3 = [pl.ds(i * (half // 2), half // 2) for i in range(4)]
    ag_ra = remote(tok.at[top], xall.at[x, top], right)
    ag_lb = remote(tok.at[bot], xall.at[x, bot], left)
    ag_rb = remote(tok.at[bot], xall.at[x, bot], right)
    ag_la = remote(tok.at[top], xall.at[x, top], left)
    for c in (ag_ra, ag_lb, ag_rb, ag_la):
        c.start()
    ag_fr = [remote(xall.at[xl, q], xall.at[xl, q], right) for q in (q1, q0)]
    ag_fl = [remote(xall.at[xr, q], xall.at[xr, q], left) for q in (q2, q3)]
    in_la = landing(ag_ra, xall.at[xl, top])
    in_rb = landing(ag_lb, xall.at[xr, bot])
    in_lb = landing(ag_rb, xall.at[xl, bot])
    in_ra = landing(ag_la, xall.at[xr, top])
    in_oa = [landing(c, xall.at[xo, q]) for c, q in zip(ag_fr, (q1, q0))]
    in_ob = [landing(c, xall.at[xo, q]) for c, q in zip(ag_fl, (q2, q3))]

    loads[0].wait()
    lane = lax.broadcasted_iota(jnp.int32, (nh, FCAP), 1)
    sub = lax.broadcasted_iota(jnp.int32, (FCAP, HD), 0)
    parts = []
    for f in range(cap // FCAP):
        n = counts[f]
        parts.append(jnp.where(lane < n, dec[:, f * FCAP:(f + 1) * FCAP], 0.0))
        liveb[f * FCAP:(f + 1) * FCAP, :] = jnp.where(sub < n, 1.0, 0.0)
    run = jnp.concatenate(parts, axis=1)
    at = lax.broadcasted_iota(jnp.int32, (nh, cap), 1)
    k = 1
    while k < cap:
        run = run + jnp.where(at >= k, pltpu.roll(run, k, axis=1), 0.0)
        k *= 2
    crow[...] = run
    for h in range(nh):
        def spread(b, _, h=h):
            at_b = pl.ds(pl.multiple_of(b * HD, HD), HD)
            ccb[h, at_b, :] = jnp.broadcast_to(crow[h:h + 1, at_b], (HD, HD)).T
            return 0
        lax.fori_loop(0, cap // HD, spread, 0)
    tot_send[...] = jnp.concatenate([ccb[h % nh, cap - 1:cap, :] for h in range(8)], axis=0)

    tot = []
    for d in range(1, NP):
        c = remote(tot_send, tot_recv.at[p], (z * NP + plane(d), x))
        c.start()
        tot.append(landing(c, tot_recv.at[plane(NP - d)]))
    tot_recv[p] = tot_send[...]

    ext = pl.ds(1, NX - 1)
    cols0, cols1 = pl.ds(0, wcol), pl.ds(wcol, wcol)
    sibling = (z * NP + y * 2 + (1 - core), x)

    def yed(d):
        return lax.rem(y + d + ny, ny)

    def at_y(d):
        return (z * NP + yed(d) * 2 + core, x)

    def at_z(d):
        return (zed(d) * NP + p, x)

    def piece0(zb, yb):
        return wg.at[ext, pl.ds(pl.multiple_of((zb * ny + yb) * wrow, wrow), wrow), cols0]

    def piece1(zb, yb):
        return wg.at[ext, pl.ds(pl.multiple_of((yb * nz + zb) * wrow, wrow), wrow), cols1]

    def block0(zb):
        return wg.at[ext, pl.ds(pl.multiple_of(zb * (ny * wrow), ny * wrow), ny * wrow), cols0]

    def block1(yb, part=None):
        n = nz * wrow
        r = yb * n
        if part is not None:
            n = n // 2
            r = r + part * n
        return wg.at[ext, pl.ds(pl.multiple_of(r, n), n), cols1]

    ups, downs = nz // 2, (nz - 1) // 2
    wy = [remote(piece0(z, y), piece0(z, y), at_y(d), 0) for d in range(1, ny)]
    wy_in = [landing(c, piece0(z, yed(-d - 1))) for d, c in enumerate(wy)]
    up = [remote(block0(zed(-s)), block0(zed(-s)), at_z(1), 0) for s in range(ups)]
    down = [remote(block0(zed(s)), block0(zed(s)), at_z(-1), 0) for s in range(downs)]
    up_in = [landing(c, block0(zed(-s - 1))) for s, c in enumerate(up)]
    down_in = [landing(c, block0(zed(s + 1))) for s, c in enumerate(down)]
    cross0 = {s: remote(block0(zed(s)), block0(zed(s)), sibling, 0) for s in range(-ups, downs + 1)}
    cross0_in = [landing(c, block0(zed(s))) for s, c in cross0.items()]

    wz = [remote(piece1(z, y), piece1(z, y), at_z(d), 1) for d in range(1, nz)]
    wz_in = [landing(c, piece1(zed(-d - 1), y)) for d, c in enumerate(wz)]
    ring_r = remote(block1(y), block1(y), at_y(1), 1)
    ring_l = remote(block1(y), block1(y), at_y(-1), 1)
    ring_r_in = landing(ring_r, block1(yed(-1)))
    ring_l_in = landing(ring_l, block1(yed(1)))
    pass_r = remote(block1(yed(-1), 0), block1(yed(-1), 0), at_y(1), 1)
    pass_l = remote(block1(yed(1), 1), block1(yed(1), 1), at_y(-1), 1)
    pass_r_in = landing(pass_r, block1(yed(2), 0))
    pass_l_in = landing(pass_l, block1(yed(2), 1))
    cross1 = {s: remote(block1(yed(s)), block1(yed(s)), sibling, 1) for s in (0, -1, 1, 2)}
    cross1_in = [landing(c, block1(yed(s))) for s, c in cross1.items()]

    def relay_w(s):
        if s == 0:
            for c in wy_in:
                c.wait_recv()
            cross0[0].start()
        else:
            up_in[s - 1].wait_recv()
            if s < ups:
                up[s].start()
            cross0[-s].start()
            if s <= downs:
                down_in[s - 1].wait_recv()
                cross0[s].start()
        if s == 0:
            up[0].start()
        if s < downs:
            down[s].start()

    for c in wx:
        c.wait_recv()

    @pl.when(core == 0)
    def _():
        for c in wy:
            c.start()

    @pl.when(core == 1)
    def _():
        for c in wz:
            c.start()

    pt = []
    for d in range(1, nz):
        c = remote(pt_send, pt_recv.at[z], at_z(d))
        pt.append((c, landing(c, pt_recv.at[zed(-d)])))

    st_acc[...] = jnp.zeros_like(st_acc)
    seg = half // 2

    def unit(u, _):
        @pl.when(u == 0)
        def _():
            loads[1].wait()
            loads[2].wait()
            loads[4].wait()

        @pl.when(u == 2)
        def _():
            @pl.when(core == 0)
            def _():
                relay_w(0)

            in_la.wait_recv()
            for c in ag_fr:
                c.start()
            in_rb.wait_recv()
            for c in ag_fl:
                c.start()

            @pl.when(core == 1)
            def _():
                for c in wz_in:
                    c.wait_recv()
                ring_r.start()
                ring_l.start()
                cross1[0].start()

            for c in tot:
                c.wait_recv()
            total = tot_recv[0]
            for j in range(1, NP):
                total = total + tot_recv[j]
            pt_send[...] = total
            pt_recv[z] = total
            for c, _ in pt:
                c.start()

        @pl.when((u == 3) & (core == 0))
        def _():
            relay_w(1)

        @pl.when(u == 4)
        def _():
            @pl.when(core == 0)
            def _():
                relay_w(2)

            in_lb.wait_recv()

        @pl.when(u == 5)
        def _():
            in_ra.wait_recv()

        @pl.when(u == 6)
        def _():
            @pl.when(core == 0)
            def _():
                relay_w(3)

            @pl.when(core == 1)
            def _():
                ring_r_in.wait_recv()
                pass_r.start()
                ring_l_in.wait_recv()
                pass_l.start()
                cross1[-1].start()
                cross1[1].start()

            in_oa[0].wait_recv()
            in_ob[0].wait_recv()

        @pl.when(u == 7)
        def _():
            in_oa[1].wait_recv()
            in_ob[1].wait_recv()

        from_left = (u == 2) | (u == 4)
        off = jnp.where(u < 2, 0, jnp.where(u > 5, 2, jnp.where(from_left, 3, 1)))
        ci = lax.rem(x + off, NX)
        low = jnp.where((u == 1) | (u == 3) | (u == 4), 2, jnp.where(u == 6, 1, 0))
        high = jnp.where(u == 7, 3, low + 1)
        step = 32

        for e, sg in enumerate((low, high)):
            def norm(i, _, e=e, sg=sg):
                src = pl.ds(pl.multiple_of(sg * seg + i * step, step), step)
                dst = pl.ds(pl.multiple_of(e * seg + i * step, step), step)
                v = xall[ci, src, :].astype(F32)
                scale = lax.rsqrt(jnp.sum(v * v, axis=1, keepdims=True) * (1.0 / width) + 1e-05)
                nrm[dst, :] = (v * scale * ngv[...]).astype(BF16)
                return 0

            lax.fori_loop(0, seg // step, norm, 0)

        segs = [pl.ds(pl.multiple_of(ci * rows + sg * seg, seg), seg) for sg in (low, high)]
        wide = 256
        for j in (1, 2, 0):
            for n in range(inn // wide):
                cols = slice(n * wide, (n + 1) * wide)
                v = _dot(nrm[...], wq[j, :, cols])
                for e, rs in enumerate(segs):
                    part = v[e * seg:(e + 1) * seg]
                    if j == 1:
                        part = part * jnp.concatenate([liveb[rs, :]] * (wide // HD), axis=1)
                    qkv[j, rs, cols] = part.astype(BF16)

        for h in range(nh):
            cols = slice(h * HD, (h + 1) * HD)
            last_c = ccb[h, cap - 1:cap, :]
            ks, vs = [], []
            for rs in segs:
                ks.append((qkv[1, rs, cols].astype(F32) * jnp.exp(last_c - ccb[h, rs, :])).astype(BF16))
                vs.append(qkv[2, rs, cols])
            st_acc[h] += _dot_tn(jnp.concatenate(ks, axis=0), jnp.concatenate(vs, axis=0))
        return 0

    lax.fori_loop(0, 8, unit, 0)

    per = HD // piece
    st = []
    for d in range(1, NP):
        c = remote(st_send.at[plane(d)], st_recv.at[p], (z * NP + plane(d), x))
        st.append((c, landing(c, st_recv.at[plane(NP - d)])))
    pls = []
    for d in range(1, nz):
        c = remote(pl_send, pl_recv.at[z], (zed(d) * NP + p, x))
        pls.append((c, landing(c, pl_recv.at[zed(-d)])))
    prs = []
    for d in range(1, NP):
        c = remote(pr_send.at[plane(d)], prior.at[p], (z * NP + plane(d), x))
        prs.append((c, landing(c, prior.at[plane(NP - d)])))
    hq = p // per

    for q in range(NP):
        st_send[q] = st_acc[q // per, (q % per) * piece:(q % per + 1) * piece, :].astype(BF16)
    for c, _ in st:
        c.start()
    st_recv[p] = st_send[p]

    tile = 256
    ri = lax.broadcasted_iota(jnp.int32, (tile, tile), 0)
    ci_ = lax.broadcasted_iota(jnp.int32, (tile, tile), 1)

    def inside(h, _):
        cols = pl.ds(pl.multiple_of(h * HD, HD), HD)
        for i in range(cap // tile):
            ra = slice(i * tile, (i + 1) * tile)
            q = qkv[0, ra, cols]
            ccol = ccb[h, ra, :]
            ccol = jnp.concatenate([ccol] * (tile // HD), axis=1)
            o = jnp.zeros((tile, HD), F32)
            for j in range(i + 1):
                sa = slice(j * tile, (j + 1) * tile)
                sc = _dot_nt(q, qkv[1, sa, cols])
                gap = ccol - crow[pl.ds(h, 1), sa]
                if i == j:
                    gap = jnp.where(ri >= ci_, gap, -1e30)
                o = o + _dot((sc * jnp.exp(gap)).astype(BF16), qkv[2, sa, cols])
            ins[ra, cols] = o

        @pl.when(h == 1)
        def _():
            for _, c in st:
                c.wait_recv()
            state = jnp.zeros((piece, HD), F32)
            for j in range(NP):
                inner[j] = state
                state = jnp.exp(tot_recv[j, pl.ds(hq, 1), :]) * state + st_recv[j].astype(F32)
            pl_send[...] = state.astype(BF16)
            for c, _ in pls:
                c.start()
            pl_recv[z] = pl_send[...]

        @pl.when(h == 2)
        def _():
            @pl.when(core == 0)
            def _():
                relay_w(4)

            @pl.when(core == 1)
            def _():
                pass_r_in.wait_recv()
                pass_l_in.wait_recv()
                cross1[2].start()

            for _, c in pt:
                c.wait_recv()
            for _, c in pls:
                c.wait_recv()
            state = jnp.zeros((piece, HD), F32)
            for j in range(nz):
                nxt = jnp.exp(pt_recv[j, pl.ds(hq, 1), :]) * state + pl_recv[j].astype(F32)
                state = jnp.where(j < z, nxt, state)
            seen = jnp.zeros((1, HD), F32)
            for j in range(NP):
                pr_send[j] = (inner[j] + jnp.exp(seen) * state).astype(BF16)
                seen = seen + tot_recv[j, pl.ds(hq, 1), :]
            for c, _ in prs:
                c.start()
            prior[p] = pr_send[p]
        return 0

    lax.fori_loop(0, nh, inside, 0)

    a2a_oa = remote(ho_s.at[2, top], relay.at[0], right)
    a2a_ob = remote(ho_s.at[2, bot], relay.at[1], left)
    a2a_r = remote(ho_s.at[1], ho_r.at[3], right)
    a2a_l = remote(ho_s.at[3], ho_r.at[1], left)
    a2a_fr = remote(relay.at[0], ho_r.at[2, top], right)
    a2a_fl = remote(relay.at[1], ho_r.at[2, bot], left)
    got_oa = landing(a2a_oa, relay.at[0])
    got_ob = landing(a2a_ob, relay.at[1])
    got_l = landing(a2a_r, ho_r.at[3])
    got_r = landing(a2a_l, ho_r.at[1])
    got_fa = landing(a2a_fr, ho_r.at[2, top])
    got_fb = landing(a2a_fl, ho_r.at[2, bot])

    loads[3].wait()
    for _, c in prs:
        c.wait_recv()

    def attended(s, _):
        off = jnp.where(s == 0, 2, jnp.where(s == 1, 1, jnp.where(s == 2, 3, 0)))
        r0 = pl.multiple_of(lax.rem(x + off, NX) * rows, rows)
        ra = pl.ds(r0, rows)
        for h in range(nh):
            cols = slice(h * HD, (h + 1) * HD)
            held = jnp.concatenate([prior[h * per + e] for e in range(per)], axis=0)
            o = ins[ra, cols] + _dot(qkv[0, ra, cols], held) * jnp.exp(ccb[h, ra, :])
            r = lax.rsqrt(jnp.sum(o * o, axis=1, keepdims=True) * (1.0 / HD) + 1e-05)
            ho_s[off, :, cols] = (o * r * hgv[:, cols]).astype(BF16)

        @pl.when(s == 0)
        def _():
            a2a_oa.start()
            a2a_ob.start()

        @pl.when(s == 1)
        def _():
            a2a_r.start()

        @pl.when(s == 2)
        def _():
            a2a_l.start()

        return 0

    lax.fori_loop(0, NX, attended, 0)
    got_oa.wait_recv()
    a2a_fr.start()
    got_ob.wait_recv()
    a2a_fl.start()

    loads[5].wait()
    wide = 512
    own = pl.multiple_of(x * rows, rows)
    lv = liveb[pl.ds(own, rows), :]
    lv = jnp.concatenate([lv] * (wide // HD), axis=1)

    def first(n, _):
        cols = pl.ds(pl.multiple_of(n * wide, wide), wide)
        acc[:, cols] = _dot(ho_s[0], wg[0, :, cols]) + xall[x, :, cols].astype(F32)
        return 0

    lax.fori_loop(0, width // wide, first, 0)

    @pl.when(core == 1)
    def _():
        for c in cross0_in:
            c.wait_recv()

    @pl.when(core == 0)
    def _():
        for c in cross1_in:
            c.wait_recv()

    def more(i, _):
        @pl.when(i == 0)
        def _():
            got_l.wait_recv()

        @pl.when(i == 1)
        def _():
            got_r.wait_recv()

        q = jnp.where(i == 0, 3, 1)

        def col(n, _):
            cols = pl.ds(pl.multiple_of(n * wide, wide), wide)
            acc[:, cols] += _dot(ho_r[q], wg[q, :, cols])
            return 0

        lax.fori_loop(0, width // wide, col, 0)
        return 0

    lax.fori_loop(0, 2, more, 0)
    got_fa.wait_recv()
    got_fb.wait_recv()

    def last(n, _):
        cols = pl.ds(pl.multiple_of(n * wide, wide), wide)
        v = acc[:, cols] + _dot(ho_r[2], wg[2, :, cols])
        out[:, cols] = (v * lv).astype(BF16)
        return 0

    lax.fori_loop(0, width // wide, last, 0)
    for c in started:
        c.wait_send()
    for who in range(2):
        @pl.when(core == who)
        def _(who=who):
            for c in by_core[who]:
                c.wait_send()


def on_device(tokens, frame_counts, decay_log, norm_gain, w_qkv, head_gain, w_out, *, nz):
    rows, width = tokens.shape
    inn = w_qkv.shape[2]
    nh = inn // HD
    cap = NX * rows
    piece = nh * HD // NP
    n_sem = 96
    vm = pltpu.VMEM
    anyspace = pl.BlockSpec(memory_space=pl.ANY)
    return pl.pallas_call(
        functools.partial(kernel, nz),
        out_shape=pltpu.VMEM((rows, width), BF16),
        in_specs=[pl.BlockSpec(memory_space=pltpu.SMEM)] + [anyspace] * 6,
        out_specs=pl.BlockSpec(memory_space=pltpu.VMEM),
        scratch_shapes=[
            vm((NX, rows, width), BF16),
            vm((rows // 2, width), BF16),
            vm((3, width, inn), BF16),
            vm((3, cap, inn), BF16),
            vm((cap, inn), F32),
            vm((NX, inn, width), BF16),
            vm((rows, width), F32),
            vm((nh, cap), F32),
            vm((nh, cap, HD), F32),
            vm((cap, HD), F32),
            vm((nh, cap), F32),
            vm((1, width), F32),
            vm((1, inn), F32),
            vm((nh, HD, HD), F32),
            vm((NP, piece, HD), BF16),
            vm((NP, piece, HD), BF16),
            vm((NP, piece, HD), F32),
            vm((piece, HD), BF16),
            vm((nz, piece, HD), BF16),
            vm((8, HD), F32),
            vm((NP, 8, HD), F32),
            vm((8, HD), F32),
            vm((nz, 8, HD), F32),
            vm((NP, piece, HD), BF16),
            vm((NP, piece, HD), BF16),
            vm((NX, rows, inn), BF16),
            vm((NX, rows, inn), BF16),
            vm((2, rows // 2, inn), BF16),
            pltpu.SemaphoreType.DMA((6,)),
            pltpu.SemaphoreType.DMA((n_sem,)),
            pltpu.SemaphoreType.DMA((n_sem,)),
        ],
        compiler_params=pltpu.CompilerParams(collective_id=0, has_side_effects=True),
        name="sublayer",
    )(
        frame_counts,
        tokens,
        decay_log,
        norm_gain.reshape(1, width),
        head_gain.reshape(1, inn),
        jnp.transpose(w_qkv, (1, 0, 2)),
        w_out,
    )


def solution(mesh):
    nz = mesh.shape[TM] // NP
    return jax.shard_map(
        functools.partial(on_device, nz=nz),
        mesh=mesh,
        in_specs=(
            P((TM, HEAD), None),
            P(TM),
            P(HEAD, TM),
            P(),
            P(None, None, HEAD),
            P(HEAD),
            P(HEAD, None),
        ),
        out_specs=P((TM, HEAD), None),
        check_vma=False,
    )
```

```python
import functools

import jax
import jax.numpy as jnp
from jax import lax
from jax.experimental import pallas as pl
from jax.experimental.pallas import tpu as pltpu
from jax.sharding import PartitionSpec as P

MESH = pl.DeviceIdType.MESH
F32 = jnp.float32
BF16 = jnp.bfloat16

FCAP = 128
HD = 128
NX = 4
NP = 8
TM, HEAD = "tm", "head"


def _dot(a, b):
    return jnp.dot(a, b, preferred_element_type=F32)


def _dot_nt(a, b):
    return lax.dot_general(a, b, (((1,), (1,)), ((), ())), preferred_element_type=F32)


def _dot_tn(a, b):
    return lax.dot_general(a, b, (((0,), (0,)), ((), ())), preferred_element_type=F32)


def kernel(
    nz, counts, tok, decay, ngain, hgain, w3, wo, out,
    xall, nrm, wq, qkv, ins, wg, acc, crow, ccb, liveb, dec, ngv, hgv,
    st_acc, st_send, st_recv, inner, pl_send, pl_recv, tot_send, tot_recv,
    pt_send, pt_recv, pr_send, prior, ho_s, ho_r, relay, lsem, ssem, rsem,
):
    rows = xall.shape[1]
    half = rows // 2
    cap = NX * rows
    width = xall.shape[2]
    inn = hgv.shape[1]
    nh = inn // HD
    piece = st_send.shape[1]
    wrow = inn // (nz * NP // 2)
    wcol = width // 2

    tm = lax.axis_index(TM)
    x = lax.axis_index(HEAD)
    z = tm // NP
    p = lax.rem(tm, NP)
    y = p // 2
    core = lax.rem(p, 2)
    xr, xo, xl = lax.rem(x + 1, NX), lax.rem(x + 2, NX), lax.rem(x + 3, NX)

    def plane(d):
        return lax.rem(p + d, NP)

    def zed(d):
        return lax.rem(z + d + nz, nz)

    loads = [
        pltpu.make_async_copy(decay, dec, lsem.at[0]),
        pltpu.make_async_copy(tok, xall.at[x], lsem.at[1]),
        pltpu.make_async_copy(ngain, ngv, lsem.at[2]),
        pltpu.make_async_copy(hgain, hgv, lsem.at[3]),
        pltpu.make_async_copy(w3, wq, lsem.at[4]),
        pltpu.make_async_copy(wo, wg.at[0], lsem.at[5]),
    ]
    for c in loads:
        c.start()

    barrier = pltpu.get_barrier_semaphore()
    for d in range(1, NX):
        pl.semaphore_signal(barrier, inc=1, device_id=(tm, lax.rem(x + d, NX)), device_id_type=MESH)
    for d in range(1, NP):
        pl.semaphore_signal(barrier, inc=1, device_id=(z * NP + plane(d), x), device_id_type=MESH)
    for d in range(1, nz):
        pl.semaphore_signal(barrier, inc=1, device_id=(zed(d) * NP + p, x), device_id_type=MESH)
    pl.semaphore_wait(barrier, NX - 1 + NP - 1 + nz - 1)

    def remote(src, dst, dev, to_send, to_recv):
        return pltpu.make_async_remote_copy(
            src_ref=src, dst_ref=dst, send_sem=ssem.at[to_send], recv_sem=rsem.at[to_recv],
            device_id=dev, device_id_type=MESH,
        )

    def arrived(ref, to_recv):
        remote(ref, ref, (tm, x), 0, to_recv).wait_recv()

    def sent(ref, to_send):
        remote(ref, ref, (tm, x), to_send, 0).wait_send()

    S_WX, S_AG, S_PASS, S_TOT, S_PT, S_ST, S_PL, S_PR, S_OPP, S_NBR, S_FWD, S_W = range(12)
    R_WX, R_LA, R_RB, R_LB, R_RA, R_O, _, R_TOT, R_PT, R_ST, R_PL, R_PR, R_OA, R_OB, R_L, R_R = range(16)
    R_F, R_CROSS, R_W = 16, 18, 19
    FAR = (4, 3, 5, 2, 6, 1, 7)

    right, left = (tm, xr), (tm, xl)
    top, bot = pl.ds(0, half), pl.ds(half, half)

    ny = NP // 2
    wcols = pl.ds(pl.multiple_of(core * wcol, wcol), wcol)
    wr0 = pl.multiple_of(((1 - core) * (z * ny + y) + core * (y * nz + z)) * wrow, wrow)
    for d in range(1, NX):
        remote(
            wo.at[pl.ds(wr0, wrow), wcols], wg.at[NX - d, pl.ds(wr0, wrow), wcols],
            (tm, lax.rem(x + d, NX)), S_WX, R_WX,
        ).start()

    q0, q1, q2, q3 = [pl.ds(i * (half // 2), half // 2) for i in range(4)]
    remote(tok.at[top], xall.at[x, top], right, S_AG, R_LA).start()
    remote(tok.at[bot], xall.at[x, bot], left, S_AG, R_RB).start()
    remote(tok.at[bot], xall.at[x, bot], right, S_AG, R_LB).start()
    remote(tok.at[top], xall.at[x, top], left, S_AG, R_RA).start()
    pass_right = [remote(xall.at[xl, q], xall.at[xl, q], right, S_PASS, R_O + i) for i, q in enumerate((q1, q0))]
    pass_left = [remote(xall.at[xr, q], xall.at[xr, q], left, S_PASS, R_O + i) for i, q in enumerate((q2, q3))]

    loads[0].wait()
    lane = lax.broadcasted_iota(jnp.int32, (nh, FCAP), 1)
    sub = lax.broadcasted_iota(jnp.int32, (FCAP, HD), 0)
    parts = []
    for f in range(cap // FCAP):
        n = counts[f]
        parts.append(jnp.where(lane < n, dec[:, f * FCAP:(f + 1) * FCAP], 0.0))
        liveb[f * FCAP:(f + 1) * FCAP, :] = jnp.where(sub < n, 1.0, 0.0)
    run = jnp.concatenate(parts, axis=1)
    at = lax.broadcasted_iota(jnp.int32, (nh, cap), 1)
    k = 1
    while k < cap:
        run = run + jnp.where(at >= k, pltpu.roll(run, k, axis=1), 0.0)
        k *= 2
    crow[...] = run
    for h in range(nh):
        def spread(b, _, h=h):
            at_b = pl.ds(pl.multiple_of(b * HD, HD), HD)
            ccb[h, at_b, :] = jnp.broadcast_to(crow[h:h + 1, at_b], (HD, HD)).T
            return 0
        lax.fori_loop(0, cap // HD, spread, 0)
    tot_send[...] = jnp.concatenate([ccb[h % nh, cap - 1:cap, :] for h in range(8)], axis=0)

    for d in FAR:
        remote(tot_send, tot_recv.at[p], (z * NP + plane(d), x), S_TOT, R_TOT).start()
    tot_recv[p] = tot_send[...]

    ext = pl.ds(1, NX - 1)
    cols0, cols1 = pl.ds(0, wcol), pl.ds(wcol, wcol)
    sibling = (z * NP + y * 2 + (1 - core), x)

    def yed(d):
        return lax.rem(y + d + ny, ny)

    def at_y(d):
        return (z * NP + yed(d) * 2 + core, x)

    def at_z(d):
        return (zed(d) * NP + p, x)

    def piece0(zb, yb):
        return wg.at[ext, pl.ds(pl.multiple_of((zb * ny + yb) * wrow, wrow), wrow), cols0]

    def piece1(zb, yb):
        return wg.at[ext, pl.ds(pl.multiple_of((yb * nz + zb) * wrow, wrow), wrow), cols1]

    def block0(zb):
        return wg.at[ext, pl.ds(pl.multiple_of(zb * (ny * wrow), ny * wrow), ny * wrow), cols0]

    def block1(yb, part=None):
        n = nz * wrow
        r = yb * n
        if part is not None:
            n = n // 2
            r = r + part * n
        return wg.at[ext, pl.ds(pl.multiple_of(r, n), n), cols1]

    ups, downs = nz // 2, (nz - 1) // 2
    zfar = sorted(range(1, nz), key=lambda d: -min(d, nz - d))
    wy = [remote(piece0(z, y), piece0(z, y), at_y(d), S_W, R_W) for d in (2, 1, 3)]
    up = [remote(block0(zed(-s)), block0(zed(-s)), at_z(1), S_W + 1, R_W + 1 + s) for s in range(ups)]
    down = [remote(block0(zed(s)), block0(zed(s)), at_z(-1), S_W + 1, R_W + 1 + s) for s in range(downs)]
    cross0 = {s: remote(block0(zed(s)), block0(zed(s)), sibling, S_W + 2, R_CROSS) for s in range(-ups, downs + 1)}

    wz = [remote(piece1(z, y), piece1(z, y), at_z(d), S_W, R_W) for d in zfar]
    ring = [remote(block1(y), block1(y), at_y(d), S_W + 1, R_W + 1) for d in (1, -1)]
    ring_on = [
        remote(block1(yed(-1), 0), block1(yed(-1), 0), at_y(1), S_W + 2, R_W + 2),
        remote(block1(yed(1), 1), block1(yed(1), 1), at_y(-1), S_W + 2, R_W + 2),
    ]
    cross1 = {s: remote(block1(yed(s)), block1(yed(s)), sibling, S_W + 3, R_CROSS) for s in (0, -1, 1, 2)}

    def wpart(n, cols):
        return wg.at[ext, pl.ds(0, n * wrow), cols]

    def relay_w(s):
        if s == 0:
            arrived(wpart(ny - 1, cols0), R_W)
        else:
            arrived(wpart(ny * (2 if s <= downs else 1), cols0), R_W + s)
        if s < ups:
            up[s].start()
        if s < downs:
            down[s].start()
        cross0[-s].start()
        if 0 < s <= downs:
            cross0[s].start()

    arrived(wg.at[ext, pl.ds(0, wrow), wcols], R_WX)

    @pl.when(core == 0)
    def _():
        for c in wy:
            c.start()

    @pl.when(core == 1)
    def _():
        for c in wz:
            c.start()

    pt = [remote(pt_send, pt_recv.at[z], at_z(d), S_PT, R_PT) for d in zfar]

    st_acc[...] = jnp.zeros_like(st_acc)
    seg = half // 2

    def unit(u, _):
        @pl.when(u == 0)
        def _():
            loads[1].wait()
            loads[2].wait()
            loads[4].wait()

        @pl.when(u == 2)
        def _():
            @pl.when(core == 0)
            def _():
                relay_w(0)

            arrived(xall.at[xl, top], R_LA)
            for c in pass_right:
                c.start()
            arrived(xall.at[xr, bot], R_RB)
            for c in pass_left:
                c.start()

            @pl.when(core == 1)
            def _():
                arrived(wpart(nz - 1, cols1), R_W)
                for c in ring:
                    c.start()
                cross1[0].start()

            arrived(tot_recv.at[pl.ds(0, NP - 1)], R_TOT)
            total = tot_recv[0]
            for j in range(1, NP):
                total = total + tot_recv[j]
            pt_send[...] = total
            pt_recv[z] = total
            for c in pt:
                c.start()

        @pl.when((u == 3) & (core == 0))
        def _():
            relay_w(1)

        @pl.when(u == 4)
        def _():
            @pl.when(core == 0)
            def _():
                relay_w(2)

            arrived(xall.at[xl, bot], R_LB)

        @pl.when(u == 5)
        def _():
            arrived(xall.at[xr, top], R_RA)

        @pl.when(u == 6)
        def _():
            @pl.when(core == 0)
            def _():
                relay_w(3)

            @pl.when(core == 1)
            def _():
                arrived(wpart(2 * nz, cols1), R_W + 1)
                for c in ring_on:
                    c.start()
                cross1[-1].start()
                cross1[1].start()

            arrived(xall.at[xo, top], R_O)

        @pl.when(u == 7)
        def _():
            arrived(xall.at[xo, top], R_O + 1)

        from_left = (u == 2) | (u == 4)
        off = jnp.where(u < 2, 0, jnp.where(u > 5, 2, jnp.where(from_left, 3, 1)))
        ci = lax.rem(x + off, NX)
        low = jnp.where((u == 1) | (u == 3) | (u == 4), 2, jnp.where(u == 6, 1, 0))
        high = jnp.where(u == 7, 3, low + 1)
        step = 32

        for e, sg in enumerate((low, high)):
            def norm(i, _, e=e, sg=sg):
                src = pl.ds(pl.multiple_of(sg * seg + i * step, step), step)
                dst = pl.ds(pl.multiple_of(e * seg + i * step, step), step)
                v = xall[ci, src, :].astype(F32)
                scale = lax.rsqrt(jnp.sum(v * v, axis=1, keepdims=True) * (1.0 / width) + 1e-05)
                nrm[dst, :] = (v * scale * ngv[...]).astype(BF16)
                return 0

            lax.fori_loop(0, seg // step, norm, 0)

        segs = [pl.ds(pl.multiple_of(ci * rows + sg * seg, seg), seg) for sg in (low, high)]
        wide = 256
        for j in (1, 2, 0):
            for n in range(inn // wide):
                cols = slice(n * wide, (n + 1) * wide)
                v = _dot(nrm[...], wq[j, :, cols])
                for e, rs in enumerate(segs):
                    part = v[e * seg:(e + 1) * seg]
                    if j == 1:
                        part = part * jnp.concatenate([liveb[rs, :]] * (wide // HD), axis=1)
                    qkv[j, rs, cols] = part.astype(BF16)

        for h in range(nh):
            cols = slice(h * HD, (h + 1) * HD)
            last_c = ccb[h, cap - 1:cap, :]
            ks, vs = [], []
            for rs in segs:
                ks.append((qkv[1, rs, cols].astype(F32) * jnp.exp(last_c - ccb[h, rs, :])).astype(BF16))
                vs.append(qkv[2, rs, cols])
            st_acc[h] += _dot_tn(jnp.concatenate(ks, axis=0), jnp.concatenate(vs, axis=0))
        return 0

    lax.fori_loop(0, 8, unit, 0)

    per = HD // piece
    st = [remote(st_send.at[plane(d)], st_recv.at[p], (z * NP + plane(d), x), S_ST, R_ST) for d in FAR]
    pls = [remote(pl_send, pl_recv.at[z], at_z(d), S_PL, R_PL) for d in zfar]
    prs = [remote(pr_send.at[plane(d)], prior.at[p], (z * NP + plane(d), x), S_PR, R_PR) for d in FAR]
    hq = p // per

    for q in range(NP):
        st_send[q] = st_acc[q // per, (q % per) * piece:(q % per + 1) * piece, :].astype(BF16)
    for c in st:
        c.start()
    st_recv[p] = st_send[p]

    tile = 256
    ri = lax.broadcasted_iota(jnp.int32, (tile, tile), 0)
    ci_ = lax.broadcasted_iota(jnp.int32, (tile, tile), 1)

    def inside(h, _):
        cols = pl.ds(pl.multiple_of(h * HD, HD), HD)
        for i in range(cap // tile):
            ra = slice(i * tile, (i + 1) * tile)
            q = qkv[0, ra, cols]
            ccol = ccb[h, ra, :]
            ccol = jnp.concatenate([ccol] * (tile // HD), axis=1)
            o = jnp.zeros((tile, HD), F32)
            for j in range(i + 1):
                sa = slice(j * tile, (j + 1) * tile)
                sc = _dot_nt(q, qkv[1, sa, cols])
                gap = ccol - crow[pl.ds(h, 1), sa]
                if i == j:
                    gap = jnp.where(ri >= ci_, gap, -1e30)
                o = o + _dot((sc * jnp.exp(gap)).astype(BF16), qkv[2, sa, cols])
            ins[ra, cols] = o

        @pl.when(h == 1)
        def _():
            arrived(st_recv.at[pl.ds(0, NP - 1)], R_ST)
            state = jnp.zeros((piece, HD), F32)
            for j in range(NP):
                inner[j] = state
                state = jnp.exp(tot_recv[j, pl.ds(hq, 1), :]) * state + st_recv[j].astype(F32)
            pl_send[...] = state.astype(BF16)
            for c in pls:
                c.start()
            pl_recv[z] = pl_send[...]

        @pl.when(h == 2)
        def _():
            @pl.when(core == 0)
            def _():
                relay_w(4)

            @pl.when(core == 1)
            def _():
                arrived(wpart(nz, cols1), R_W + 2)
                cross1[2].start()

            arrived(pt_recv.at[pl.ds(0, nz - 1)], R_PT)
            arrived(pl_recv.at[pl.ds(0, nz - 1)], R_PL)
            state = jnp.zeros((piece, HD), F32)
            for j in range(nz):
                nxt = jnp.exp(pt_recv[j, pl.ds(hq, 1), :]) * state + pl_recv[j].astype(F32)
                state = jnp.where(j < z, nxt, state)
            seen = jnp.zeros((1, HD), F32)
            for j in range(NP):
                pr_send[j] = (inner[j] + jnp.exp(seen) * state).astype(BF16)
                seen = seen + tot_recv[j, pl.ds(hq, 1), :]
            for c in prs:
                c.start()
            prior[p] = pr_send[p]
        return 0

    lax.fori_loop(0, nh, inside, 0)

    hcols = [pl.ds(i * (inn // 2), inn // 2) for i in range(2)]
    a2a_oa = remote(ho_s.at[2, top], relay.at[0], right, S_OPP, R_OA)
    a2a_ob = remote(ho_s.at[2, bot], relay.at[1], left, S_OPP, R_OB)
    a2a_r = remote(ho_s.at[1], ho_r.at[3], right, S_NBR, R_L)
    a2a_l = remote(ho_s.at[3], ho_r.at[1], left, S_NBR, R_R)
    on_right = [remote(relay.at[0, :, c], ho_r.at[2, top, c], right, S_FWD, R_F + i) for i, c in enumerate(hcols)]
    on_left = [remote(relay.at[1, :, c], ho_r.at[2, bot, c], left, S_FWD, R_F + i) for i, c in enumerate(hcols)]

    loads[3].wait()
    arrived(prior.at[pl.ds(0, NP - 1)], R_PR)

    def attended(s, _):
        off = jnp.where(s == 0, 2, jnp.where(s == 1, 1, jnp.where(s == 2, 3, 0)))
        r0 = pl.multiple_of(lax.rem(x + off, NX) * rows, rows)
        ra = pl.ds(r0, rows)
        for h in range(nh):
            cols = slice(h * HD, (h + 1) * HD)
            held = jnp.concatenate([prior[h * per + e] for e in range(per)], axis=0)
            o = ins[ra, cols] + _dot(qkv[0, ra, cols], held) * jnp.exp(ccb[h, ra, :])
            r = lax.rsqrt(jnp.sum(o * o, axis=1, keepdims=True) * (1.0 / HD) + 1e-05)
            ho_s[off, :, cols] = (o * r * hgv[:, cols]).astype(BF16)

        @pl.when(s == 0)
        def _():
            a2a_oa.start()
            a2a_ob.start()

        @pl.when(s == 1)
        def _():
            a2a_r.start()

        @pl.when(s == 2)
        def _():
            a2a_l.start()

        return 0

    lax.fori_loop(0, NX, attended, 0)
    arrived(relay.at[0], R_OA)
    for c in on_right:
        c.start()
    arrived(relay.at[1], R_OB)
    for c in on_left:
        c.start()

    loads[5].wait()
    wide = 512
    own = pl.multiple_of(x * rows, rows)
    lv = liveb[pl.ds(own, rows), :]
    lv = jnp.concatenate([lv] * (wide // HD), axis=1)

    def first(n, _):
        cols = pl.ds(pl.multiple_of(n * wide, wide), wide)
        acc[:, cols] = _dot(ho_s[0], wg[0, :, cols]) + xall[x, :, cols].astype(F32)
        return 0

    lax.fori_loop(0, width // wide, first, 0)
    arrived(wg.at[ext, :, pl.ds(0, wcol)], R_CROSS)

    def more(i, _):
        @pl.when(i == 0)
        def _():
            arrived(ho_r.at[3], R_L)

        @pl.when(i == 1)
        def _():
            arrived(ho_r.at[1], R_R)

        q = jnp.where(i == 0, 3, 1)

        def col(n, _):
            cols = pl.ds(pl.multiple_of(n * wide, wide), wide)
            acc[:, cols] += _dot(ho_r[q], wg[q, :, cols])
            return 0

        lax.fori_loop(0, width // wide, col, 0)
        return 0

    lax.fori_loop(0, 2, more, 0)
    k0, k1 = slice(0, inn // 2), slice(inn // 2, inn)
    arrived(relay.at[:, :, hcols[0]], R_F)

    def first_half(n, _):
        cols = pl.ds(pl.multiple_of(n * wide, wide), wide)
        acc[:, cols] += _dot(ho_r[2, :, k0], wg[2, k0, cols])
        return 0

    lax.fori_loop(0, width // wide, first_half, 0)
    arrived(relay.at[:, :, hcols[1]], R_F + 1)

    def last(n, _):
        cols = pl.ds(pl.multiple_of(n * wide, wide), wide)
        v = acc[:, cols] + _dot(ho_r[2, :, k1], wg[2, k1, cols])
        out[:, cols] = (v * lv).astype(BF16)
        return 0

    lax.fori_loop(0, width // wide, last, 0)

    sent(wg.at[ext, pl.ds(0, wrow), wcols], S_WX)
    sent(xall.at[pl.ds(0, 2)], S_AG)
    sent(xall.at[0], S_PASS)
    sent(tot_recv.at[pl.ds(0, NP - 1)], S_TOT)
    sent(pt_recv.at[pl.ds(0, nz - 1)], S_PT)
    sent(st_recv.at[pl.ds(0, NP - 1)], S_ST)
    sent(pl_recv.at[pl.ds(0, nz - 1)], S_PL)
    sent(prior.at[pl.ds(0, NP - 1)], S_PR)
    sent(relay, S_OPP)
    sent(ho_r.at[pl.ds(0, 2)], S_NBR)
    sent(relay, S_FWD)

    @pl.when(core == 0)
    def _():
        sent(wpart(ny - 1, cols0), S_W)
        sent(wpart((nz - 1) * ny, cols0), S_W + 1)
        sent(wpart(nz * ny, cols0), S_W + 2)

    @pl.when(core == 1)
    def _():
        sent(wpart(nz - 1, cols1), S_W)
        sent(wpart(2 * nz, cols1), S_W + 1)
        sent(wpart(nz, cols1), S_W + 2)
        sent(wpart(nz * ny, cols1), S_W + 3)


def on_device(tokens, frame_counts, decay_log, norm_gain, w_qkv, head_gain, w_out, *, nz):
    rows, width = tokens.shape
    inn = w_qkv.shape[2]
    nh = inn // HD
    cap = NX * rows
    piece = nh * HD // NP
    vm = pltpu.VMEM
    anyspace = pl.BlockSpec(memory_space=pl.ANY)
    return pl.pallas_call(
        functools.partial(kernel, nz),
        out_shape=pltpu.VMEM((rows, width), BF16),
        in_specs=[pl.BlockSpec(memory_space=pltpu.SMEM)] + [anyspace] * 6,
        out_specs=pl.BlockSpec(memory_space=pltpu.VMEM),
        scratch_shapes=[
            vm((NX, rows, width), BF16),
            vm((rows // 2, width), BF16),
            vm((3, width, inn), BF16),
            vm((3, cap, inn), BF16),
            vm((cap, inn), F32),
            vm((NX, inn, width), BF16),
            vm((rows, width), F32),
            vm((nh, cap), F32),
            vm((nh, cap, HD), F32),
            vm((cap, HD), F32),
            vm((nh, cap), F32),
            vm((1, width), F32),
            vm((1, inn), F32),
            vm((nh, HD, HD), F32),
            vm((NP, piece, HD), BF16),
            vm((NP, piece, HD), BF16),
            vm((NP, piece, HD), F32),
            vm((piece, HD), BF16),
            vm((nz, piece, HD), BF16),
            vm((8, HD), F32),
            vm((NP, 8, HD), F32),
            vm((8, HD), F32),
            vm((nz, 8, HD), F32),
            vm((NP, piece, HD), BF16),
            vm((NP, piece, HD), BF16),
            vm((NX, rows, inn), BF16),
            vm((NX, rows, inn), BF16),
            vm((2, rows // 2, inn), BF16),
            pltpu.SemaphoreType.DMA((6,)),
            pltpu.SemaphoreType.DMA((15,)),
            pltpu.SemaphoreType.DMA((20 + nz // 2,)),
        ],
        compiler_params=pltpu.CompilerParams(collective_id=0, has_side_effects=True),
        name="sublayer",
    )(
        frame_counts,
        tokens,
        decay_log,
        norm_gain.reshape(1, width),
        head_gain.reshape(1, inn),
        jnp.transpose(w_qkv, (1, 0, 2)),
        w_out,
    )


def solution(mesh):
    nz = mesh.shape[TM] // NP
    return jax.shard_map(
        functools.partial(on_device, nz=nz),
        mesh=mesh,
        in_specs=(
            P((TM, HEAD), None),
            P(TM),
            P(HEAD, TM),
            P(),
            P(None, None, HEAD),
            P(HEAD),
            P(HEAD, None),
        ),
        out_specs=P((TM, HEAD), None),
        check_vma=False,
    )
```

```python
import functools

import jax
import jax.numpy as jnp
from jax import lax
from jax.experimental import pallas as pl
from jax.experimental.pallas import tpu as pltpu
from jax.sharding import PartitionSpec as P

MESH = pl.DeviceIdType.MESH
F32 = jnp.float32
BF16 = jnp.bfloat16

FCAP = 128
HD = 128
NX = 4
NP = 8
TM, HEAD = "tm", "head"


def _dot(a, b):
    return jnp.dot(a, b, preferred_element_type=F32)


def _dot_nt(a, b):
    return lax.dot_general(a, b, (((1,), (1,)), ((), ())), preferred_element_type=F32)


def _dot_tn(a, b):
    return lax.dot_general(a, b, (((0,), (0,)), ((), ())), preferred_element_type=F32)


def kernel(
    nz, cnt, tok, decay, ngain, hgain, w3, wo, out,
    counts, xall, nrm, wq, qkv, ins, wg, acc, crow, ccb, liveb, dec, ngv, hgv,
    st_acc, st_send, st_recv, inner, coef, pl_send, pl_recv, tot_send, tot_recv,
    pt_send, pt_recv, pr_send, prior, ho_s, ho_r, relay, lsem, ssem, rsem,
):
    rows = xall.shape[1]
    half = rows // 2
    cap = NX * rows
    width = xall.shape[2]
    inn = hgv.shape[1]
    nh = inn // HD
    piece = st_send.shape[1]
    wrow = inn // (nz * NP // 2)
    wcol = width // 2

    tm = lax.axis_index(TM)
    x = lax.axis_index(HEAD)
    z = tm // NP
    p = lax.rem(tm, NP)
    y = p // 2
    core = lax.rem(p, 2)
    xr, xo, xl = lax.rem(x + 1, NX), lax.rem(x + 2, NX), lax.rem(x + 3, NX)

    def plane(d):
        return lax.rem(p + d, NP)

    def zed(d):
        return lax.rem(z + d + nz, nz)

    barrier = pltpu.get_barrier_semaphore()
    for d in range(1, NX):
        pl.semaphore_signal(barrier, inc=1, device_id=(tm, lax.rem(x + d, NX)), device_id_type=MESH)
    for d in range(1, NP):
        pl.semaphore_signal(barrier, inc=1, device_id=(z * NP + plane(d), x), device_id_type=MESH)
    for d in range(1, nz):
        pl.semaphore_signal(barrier, inc=1, device_id=(zed(d) * NP + p, x), device_id_type=MESH)

    loads = [
        pltpu.make_async_copy(decay, dec, lsem.at[0]),
        pltpu.make_async_copy(tok, xall.at[x], lsem.at[1]),
        pltpu.make_async_copy(ngain, ngv, lsem.at[2]),
        pltpu.make_async_copy(hgain, hgv, lsem.at[3]),
        pltpu.make_async_copy(w3, wq, lsem.at[4]),
        pltpu.make_async_copy(wo, wg.at[0], lsem.at[5]),
        pltpu.make_async_copy(cnt, counts, lsem.at[6]),
    ]
    for c in loads:
        c.start()

    pl.semaphore_wait(barrier, NX - 1 + NP - 1 + nz - 1)

    def remote(src, dst, dev, to_send, to_recv):
        return pltpu.make_async_remote_copy(
            src_ref=src, dst_ref=dst, send_sem=ssem.at[to_send], recv_sem=rsem.at[to_recv],
            device_id=dev, device_id_type=MESH,
        )

    def arrived(ref, to_recv):
        remote(ref, ref, (tm, x), 0, to_recv).wait_recv()

    def sent(ref, to_send):
        remote(ref, ref, (tm, x), to_send, 0).wait_send()

    S_WX, S_AG, S_PASS, S_TOT, S_PT, S_ST, S_PL, S_PR, S_OPP, S_NBR, S_FWD, S_W = range(12)
    R_WX, R_LA, R_RB, R_LB, R_RA, R_O, _, R_TOT, R_PT, R_ST, R_PL, R_PR, R_OA, R_OB, R_N, _ = range(16)
    R_F, R_CROSS, R_W = 16, 18, 19
    FAR = (4, 3, 5, 2, 6, 1, 7)

    right, left = (tm, xr), (tm, xl)
    top, bot = pl.ds(0, half), pl.ds(half, half)

    ny = NP // 2
    wcols = pl.ds(pl.multiple_of(core * wcol, wcol), wcol)
    wr0 = pl.multiple_of(((1 - core) * (z * ny + y) + core * (y * nz + z)) * wrow, wrow)
    for d in range(1, NX):
        remote(
            wo.at[pl.ds(wr0, wrow), wcols], wg.at[NX - d, pl.ds(wr0, wrow), wcols],
            (tm, lax.rem(x + d, NX)), S_WX, R_WX,
        ).start()

    q0, q1, q2, q3 = [pl.ds(i * (half // 2), half // 2) for i in range(4)]
    remote(tok.at[top], xall.at[x, top], right, S_AG, R_LA).start()
    remote(tok.at[bot], xall.at[x, bot], left, S_AG, R_RB).start()
    remote(tok.at[bot], xall.at[x, bot], right, S_AG, R_LB).start()
    remote(tok.at[top], xall.at[x, top], left, S_AG, R_RA).start()
    pass_right = [remote(xall.at[xl, q], xall.at[xl, q], right, S_PASS, R_O + i) for i, q in enumerate((q1, q0))]
    pass_left = [remote(xall.at[xr, q], xall.at[xr, q], left, S_PASS, R_O + i) for i, q in enumerate((q2, q3))]

    loads[0].wait()
    loads[6].wait()
    lane = lax.broadcasted_iota(jnp.int32, (nh, FCAP), 1)
    sub = lax.broadcasted_iota(jnp.int32, (FCAP, HD), 0)
    parts = []
    for f in range(cap // FCAP):
        n = counts[f]
        parts.append(jnp.where(lane < n, dec[:, f * FCAP:(f + 1) * FCAP], 0.0))
        liveb[f * FCAP:(f + 1) * FCAP, :] = jnp.where(sub < n, 1.0, 0.0)
    run = jnp.concatenate(parts, axis=1)
    at = lax.broadcasted_iota(jnp.int32, (nh, cap), 1)
    k = 1
    while k < cap:
        run = run + jnp.where(at >= k, pltpu.roll(run, k, axis=1), 0.0)
        k *= 2
    crow[...] = run
    for h in range(nh):
        def spread(b, _, h=h):
            at_b = pl.ds(pl.multiple_of(b * HD, HD), HD)
            ccb[h, at_b, :] = jnp.broadcast_to(crow[h:h + 1, at_b], (HD, HD)).T
            return 0
        lax.fori_loop(0, cap // HD, spread, 0)
    tot_send[...] = jnp.concatenate([ccb[h % nh, cap - 1:cap, :] for h in range(8)], axis=0)

    for d in FAR:
        remote(tot_send, tot_recv.at[p], (z * NP + plane(d), x), S_TOT, R_TOT).start()
    tot_recv[p] = tot_send[...]

    ext = pl.ds(1, NX - 1)
    cols0, cols1 = pl.ds(0, wcol), pl.ds(wcol, wcol)
    sibling = (z * NP + y * 2 + (1 - core), x)

    def yed(d):
        return lax.rem(y + d + ny, ny)

    def at_y(d):
        return (z * NP + yed(d) * 2 + core, x)

    def at_z(d):
        return (zed(d) * NP + p, x)

    def piece0(zb, yb):
        return wg.at[ext, pl.ds(pl.multiple_of((zb * ny + yb) * wrow, wrow), wrow), cols0]

    def piece1(zb, yb):
        return wg.at[ext, pl.ds(pl.multiple_of((yb * nz + zb) * wrow, wrow), wrow), cols1]

    def block0(zb):
        return wg.at[ext, pl.ds(pl.multiple_of(zb * (ny * wrow), ny * wrow), ny * wrow), cols0]

    def block1(yb, part=None):
        n = nz * wrow
        r = yb * n
        if part is not None:
            n = n // 2
            r = r + part * n
        return wg.at[ext, pl.ds(pl.multiple_of(r, n), n), cols1]

    ups, downs = nz // 2, (nz - 1) // 2
    zfar = sorted(range(1, nz), key=lambda d: -min(d, nz - d))
    wy = [remote(piece0(z, y), piece0(z, y), at_y(d), S_W, R_W) for d in (2, 1, 3)]
    up = [remote(block0(zed(-s)), block0(zed(-s)), at_z(1), S_W + 1, R_W + 1 + s) for s in range(ups)]
    down = [remote(block0(zed(s)), block0(zed(s)), at_z(-1), S_W + 1, R_W + 1 + s) for s in range(downs)]
    cross0 = {s: remote(block0(zed(s)), block0(zed(s)), sibling, S_W + 2, R_CROSS) for s in range(-ups, downs + 1)}

    wz = [remote(piece1(z, y), piece1(z, y), at_z(d), S_W, R_W) for d in zfar]
    ring = [remote(block1(y), block1(y), at_y(d), S_W + 1, R_W + 1) for d in (1, -1)]
    ring_on = [
        remote(block1(yed(-1), 0), block1(yed(-1), 0), at_y(1), S_W + 2, R_W + 2),
        remote(block1(yed(1), 1), block1(yed(1), 1), at_y(-1), S_W + 2, R_W + 2),
    ]
    cross1 = {s: remote(block1(yed(s)), block1(yed(s)), sibling, S_W + 3, R_CROSS) for s in (0, -1, 1, 2)}

    def wpart(n, cols):
        return wg.at[ext, pl.ds(0, n * wrow), cols]

    def relay_w(s):
        if s == 0:
            arrived(wpart(ny - 1, cols0), R_W)
        else:
            arrived(wpart(ny * (2 if s <= downs else 1), cols0), R_W + s)
        if s < ups:
            up[s].start()
        if s < downs:
            down[s].start()
        cross0[-s].start()
        if 0 < s <= downs:
            cross0[s].start()

    arrived(wg.at[ext, pl.ds(0, wrow), wcols], R_WX)

    @pl.when(core == 0)
    def _():
        for c in wy:
            c.start()

    @pl.when(core == 1)
    def _():
        for c in wz:
            c.start()

    pt = [remote(pt_send, pt_recv.at[z], at_z(d), S_PT, R_PT) for d in zfar]

    st = [remote(st_send.at[plane(d)], st_recv.at[p], (z * NP + plane(d), x), S_ST, R_ST) for d in FAR]
    pls = [remote(pl_send, pl_recv.at[z], at_z(d), S_PL, R_PL) for d in zfar]
    prs = [remote(pr_send.at[plane(d)], prior.at[p], (z * NP + plane(d), x), S_PR, R_PR) for d in FAR]


    st_acc[...] = jnp.zeros_like(st_acc)
    UNITS = 8
    seg = half // 2
    per = HD // piece
    hq = p // per

    def unit(u, _):
        @pl.when(u == 0)
        def _():
            loads[1].wait()
            loads[2].wait()
            loads[4].wait()

        @pl.when(u == 2)
        def _():
            @pl.when(core == 0)
            def _():
                relay_w(0)

            arrived(xall.at[xl, top], R_LA)
            for c in pass_right:
                c.start()
            arrived(xall.at[xr, bot], R_RB)
            for c in pass_left:
                c.start()

            @pl.when(core == 1)
            def _():
                arrived(wpart(nz - 1, cols1), R_W)
                for c in ring:
                    c.start()
                cross1[0].start()

            arrived(tot_recv.at[pl.ds(0, NP - 1)], R_TOT)
            total = tot_recv[0]
            for j in range(1, NP):
                total = total + tot_recv[j]
            pt_send[...] = total
            pt_recv[z] = total
            for c in pt:
                c.start()
            after = jnp.zeros((1, HD), F32)
            for j in reversed(range(NP)):
                coef[j] = jnp.exp(after)
                after = after + tot_recv[j, pl.ds(hq, 1), :]
            before = jnp.zeros((1, HD), F32)
            for j in range(NP):
                coef[NP + j] = jnp.exp(before)
                before = before + tot_recv[j, pl.ds(hq, 1), :]

        @pl.when((u == 3) & (core == 0))
        def _():
            relay_w(1)

        @pl.when(u == 4)
        def _():
            @pl.when(core == 0)
            def _():
                relay_w(2)

            arrived(xall.at[xl, bot], R_LB)

        @pl.when(u == 5)
        def _():
            arrived(xall.at[xr, top], R_RA)

        @pl.when(u == 6)
        def _():
            @pl.when(core == 0)
            def _():
                relay_w(3)

            @pl.when(core == 1)
            def _():
                arrived(wpart(2 * nz, cols1), R_W + 1)
                for c in ring_on:
                    c.start()
                cross1[-1].start()
                cross1[1].start()

            arrived(xall.at[xo, top], R_O)

        @pl.when(u == 7)
        def _():
            arrived(pt_recv.at[pl.ds(0, nz - 1)], R_PT)
            after = jnp.zeros((1, HD), F32)
            for j in reversed(range(nz)):
                coef[2 * NP + j] = jnp.where(j < z, jnp.exp(after), 0.0)
                after = after + jnp.where(j < z, pt_recv[j, pl.ds(hq, 1), :], 0.0)
            arrived(xall.at[xo, top], R_O + 1)

        from_left = (u == 2) | (u == 4)
        off = jnp.where(u < 2, 0, jnp.where(u > 5, 2, jnp.where(from_left, 3, 1)))
        ci = lax.rem(x + off, NX)
        low = jnp.where((u == 1) | (u == 3) | (u == 4), 2, jnp.where(u == 6, 1, 0))
        high = jnp.where(u == 7, 3, low + 1)
        step = 32

        for e, sg in enumerate((low, high)):
            def norm(i, _, e=e, sg=sg):
                src = pl.ds(pl.multiple_of(sg * seg + i * step, step), step)
                dst = pl.ds(pl.multiple_of(e * seg + i * step, step), step)
                v = xall[ci, src, :].astype(F32)
                scale = lax.rsqrt(jnp.sum(v * v, axis=1, keepdims=True) * (1.0 / width) + 1e-05)
                nrm[dst, :] = (v * scale * ngv[...]).astype(BF16)
                return 0

            lax.fori_loop(0, seg // step, norm, 0, unroll=True)

        segs = [pl.ds(pl.multiple_of(ci * rows + sg * seg, seg), seg) for sg in (low, high)]
        wide = 256

        def project(j):
            for n in range(inn // wide):
                cols = slice(n * wide, (n + 1) * wide)
                v = _dot(nrm[...], wq[j, :, cols])
                for e, rs in enumerate(segs):
                    part = v[e * seg:(e + 1) * seg]
                    if j == 1:
                        part = part * jnp.concatenate([liveb[rs, :]] * (wide // HD), axis=1)
                    qkv[j, rs, cols] = part.astype(BF16)

        project(1)
        project(2)
        for h in range(nh):
            cols = slice(h * HD, (h + 1) * HD)
            last_c = ccb[h, cap - 1:cap, :]
            ks, vs = [], []
            for rs in segs:
                ks.append((qkv[1, rs, cols].astype(F32) * jnp.exp(last_c - ccb[h, rs, :])).astype(BF16))
                vs.append(qkv[2, rs, cols])
            st_acc[h] += _dot_tn(jnp.concatenate(ks, axis=0), jnp.concatenate(vs, axis=0))

        @pl.when(u == UNITS - 1)
        def _():
            for q in range(NP):
                st_send[q] = st_acc[q // per, (q % per) * piece:(q % per + 1) * piece, :].astype(BF16)
            for c in st:
                c.start()
            st_recv[p] = st_send[p]

        project(0)
        return 0

    lax.fori_loop(0, UNITS, unit, 0)

    tile = 256
    ri = lax.broadcasted_iota(jnp.int32, (tile, tile), 0)
    ci_ = lax.broadcasted_iota(jnp.int32, (tile, tile), 1)

    def inside(h, _):
        cols = pl.ds(pl.multiple_of(h * HD, HD), HD)
        for i in range(cap // tile):
            ra = slice(i * tile, (i + 1) * tile)
            q = qkv[0, ra, cols]
            ccol = ccb[h, ra, :]
            ccol = jnp.concatenate([ccol] * (tile // HD), axis=1)
            o = jnp.zeros((tile, HD), F32)
            for j in range(i + 1):
                sa = slice(j * tile, (j + 1) * tile)
                sc = _dot_nt(q, qkv[1, sa, cols])
                gap = ccol - crow[pl.ds(h, 1), sa]
                if i == j:
                    gap = jnp.where(ri >= ci_, gap, -1e30)
                o = o + _dot((sc * jnp.exp(gap)).astype(BF16), qkv[2, sa, cols])
            ins[ra, cols] = o

        @pl.when(h == 1)
        def _():
            arrived(st_recv.at[pl.ds(0, NP - 1)], R_ST)
            terms = [coef[j] * st_recv[j].astype(F32) for j in range(NP)]
            while len(terms) > 1:
                terms = [u + v for u, v in zip(terms[::2], terms[1::2])]
            pl_send[...] = terms[0].astype(BF16)
            for c in pls:
                c.start()
            pl_recv[z] = pl_send[...]
            state = jnp.zeros((piece, HD), F32)
            for j in range(NP):
                inner[j] = state
                state = jnp.exp(tot_recv[j, pl.ds(hq, 1), :]) * state + st_recv[j].astype(F32)

        @pl.when(h == 2)
        def _():
            @pl.when(core == 0)
            def _():
                relay_w(4)

            @pl.when(core == 1)
            def _():
                arrived(wpart(nz, cols1), R_W + 2)
                cross1[2].start()

            arrived(pl_recv.at[pl.ds(0, nz - 1)], R_PL)
            terms = [coef[2 * NP + j] * pl_recv[j].astype(F32) for j in range(nz)]
            while len(terms) > 1:
                terms = [u + v for u, v in zip(terms[::2], terms[1::2])] + terms[len(terms) // 2 * 2:]
            for j in range(NP):
                pr_send[j] = (inner[j] + coef[NP + j] * terms[0]).astype(BF16)
            for c in prs:
                c.start()
            prior[p] = pr_send[p]
        return 0

    lax.fori_loop(0, nh, inside, 0)

    hcols = [pl.ds(i * (inn // 2), inn // 2) for i in range(2)]
    a2a_oa = remote(ho_s.at[2, top], relay.at[0], right, S_OPP, R_OA)
    a2a_ob = remote(ho_s.at[2, bot], relay.at[1], left, S_OPP, R_OB)
    a2a_r = [remote(ho_s.at[1, :, c], ho_r.at[3, :, c], right, S_NBR, R_N + i) for i, c in enumerate(hcols)]
    a2a_l = [remote(ho_s.at[3, :, c], ho_r.at[1, :, c], left, S_NBR, R_N + i) for i, c in enumerate(hcols)]
    on_right = [remote(relay.at[0, :, c], ho_r.at[2, top, c], right, S_FWD, R_F + i) for i, c in enumerate(hcols)]
    on_left = [remote(relay.at[1, :, c], ho_r.at[2, bot, c], left, S_FWD, R_F + i) for i, c in enumerate(hcols)]

    loads[3].wait()
    arrived(prior.at[pl.ds(0, NP - 1)], R_PR)

    def attended(i, _):
        s = i // 2
        off = jnp.where(s == 0, 2, jnp.where(s == 1, 1, jnp.where(s == 2, 3, 0)))
        h0 = pl.multiple_of(lax.rem(i, 2) * half, half)
        ra = pl.ds(pl.multiple_of(lax.rem(x + off, NX) * rows + h0, half), half)
        for h in range(nh):
            cols = slice(h * HD, (h + 1) * HD)
            held = jnp.concatenate([prior[h * per + e] for e in range(per)], axis=0)
            o = ins[ra, cols] + _dot(qkv[0, ra, cols], held) * jnp.exp(ccb[h, ra, :])
            r = lax.rsqrt(jnp.sum(o * o, axis=1, keepdims=True) * (1.0 / HD) + 1e-05)
            ho_s[off, pl.ds(h0, half), cols] = (o * r * hgv[:, cols]).astype(BF16)

        @pl.when(i == 0)
        def _():
            a2a_oa.start()

        @pl.when(i == 1)
        def _():
            a2a_ob.start()

        @pl.when(i == 3)
        def _():
            for c in a2a_r:
                c.start()

        @pl.when(i == 5)
        def _():
            for c in a2a_l:
                c.start()

        return 0

    lax.fori_loop(0, 2 * NX, attended, 0)
    arrived(relay.at[0], R_OA)
    for c in on_right:
        c.start()
    arrived(relay.at[1], R_OB)
    for c in on_left:
        c.start()

    loads[5].wait()
    wide = 512
    own = pl.multiple_of(x * rows, rows)
    lv = liveb[pl.ds(own, rows), :]
    lv = jnp.concatenate([lv] * (wide // HD), axis=1)

    def first(n, _):
        cols = pl.ds(pl.multiple_of(n * wide, wide), wide)
        acc[:, cols] = _dot(ho_s[0], wg[0, :, cols]) + xall[x, :, cols].astype(F32)
        return 0

    lax.fori_loop(0, width // wide, first, 0)
    arrived(wg.at[ext, :, pl.ds(0, wcol)], R_CROSS)

    k0, k1 = slice(0, inn // 2), slice(inn // 2, inn)
    for i, ks in enumerate((k0, k1)):
        arrived(ho_r.at[0], R_N + i)

        def both(n, _, ks=ks):
            cols = pl.ds(pl.multiple_of(n * wide, wide), wide)
            acc[:, cols] += _dot(ho_r[3, :, ks], wg[3, ks, cols]) + _dot(ho_r[1, :, ks], wg[1, ks, cols])
            return 0

        lax.fori_loop(0, width // wide, both, 0)
    arrived(relay.at[:, :, hcols[0]], R_F)

    def first_half(n, _):
        cols = pl.ds(pl.multiple_of(n * wide, wide), wide)
        acc[:, cols] += _dot(ho_r[2, :, k0], wg[2, k0, cols])
        return 0

    lax.fori_loop(0, width // wide, first_half, 0)
    arrived(relay.at[:, :, hcols[1]], R_F + 1)

    def last(n, _):
        cols = pl.ds(pl.multiple_of(n * wide, wide), wide)
        v = acc[:, cols] + _dot(ho_r[2, :, k1], wg[2, k1, cols])
        out[:, cols] = (v * lv).astype(BF16)
        return 0

    lax.fori_loop(0, width // wide, last, 0)

    sent(wg.at[ext, pl.ds(0, wrow), wcols], S_WX)
    sent(xall.at[pl.ds(0, 2)], S_AG)
    sent(xall.at[0], S_PASS)
    sent(tot_recv.at[pl.ds(0, NP - 1)], S_TOT)
    sent(pt_recv.at[pl.ds(0, nz - 1)], S_PT)
    sent(st_recv.at[pl.ds(0, NP - 1)], S_ST)
    sent(pl_recv.at[pl.ds(0, nz - 1)], S_PL)
    sent(prior.at[pl.ds(0, NP - 1)], S_PR)
    sent(relay, S_OPP)
    sent(ho_r.at[pl.ds(0, 2)], S_NBR)
    sent(relay, S_FWD)

    @pl.when(core == 0)
    def _():
        sent(wpart(ny - 1, cols0), S_W)
        sent(wpart((nz - 1) * ny, cols0), S_W + 1)
        sent(wpart(nz * ny, cols0), S_W + 2)

    @pl.when(core == 1)
    def _():
        sent(wpart(nz - 1, cols1), S_W)
        sent(wpart(2 * nz, cols1), S_W + 1)
        sent(wpart(nz, cols1), S_W + 2)
        sent(wpart(nz * ny, cols1), S_W + 3)


def on_device(tokens, frame_counts, decay_log, norm_gain, w_qkv, head_gain, w_out, *, nz):
    rows, width = tokens.shape
    inn = w_qkv.shape[2]
    nh = inn // HD
    cap = NX * rows
    piece = nh * HD // NP
    vm = pltpu.VMEM
    anyspace = pl.BlockSpec(memory_space=pl.ANY)
    return pl.pallas_call(
        functools.partial(kernel, nz),
        out_shape=pltpu.VMEM((rows, width), BF16),
        in_specs=[anyspace] * 7,
        out_specs=pl.BlockSpec(memory_space=pltpu.VMEM),
        scratch_shapes=[
            pltpu.SMEM(frame_counts.shape, jnp.int32),
            vm((NX, rows, width), BF16),
            vm((rows // 2, width), BF16),
            vm((3, width, inn), BF16),
            vm((3, cap, inn), BF16),
            vm((cap, inn), F32),
            vm((NX, inn, width), BF16),
            vm((rows, width), F32),
            vm((nh, cap), F32),
            vm((nh, cap, HD), F32),
            vm((cap, HD), F32),
            vm((nh, cap), F32),
            vm((1, width), F32),
            vm((1, inn), F32),
            vm((nh, HD, HD), F32),
            vm((NP, piece, HD), BF16),
            vm((NP, piece, HD), BF16),
            vm((NP, piece, HD), F32),
            vm((2 * NP + nz, 1, HD), F32),
            vm((piece, HD), BF16),
            vm((nz, piece, HD), BF16),
            vm((8, HD), F32),
            vm((NP, 8, HD), F32),
            vm((8, HD), F32),
            vm((nz, 8, HD), F32),
            vm((NP, piece, HD), BF16),
            vm((NP, piece, HD), BF16),
            vm((NX, rows, inn), BF16),
            vm((NX, rows, inn), BF16),
            vm((2, rows // 2, inn), BF16),
            pltpu.SemaphoreType.DMA((7,)),
            pltpu.SemaphoreType.DMA((15,)),
            pltpu.SemaphoreType.DMA((20 + nz // 2,)),
        ],
        compiler_params=pltpu.CompilerParams(collective_id=0, has_side_effects=True),
        name="sublayer",
    )(
        frame_counts,
        tokens,
        decay_log,
        norm_gain.reshape(1, width),
        head_gain.reshape(1, inn),
        jnp.transpose(w_qkv, (1, 0, 2)),
        w_out,
    )


def solution(mesh):
    nz = mesh.shape[TM] // NP
    return jax.shard_map(
        functools.partial(on_device, nz=nz),
        mesh=mesh,
        in_specs=(
            P((TM, HEAD), None),
            P(TM),
            P(HEAD, TM),
            P(),
            P(None, None, HEAD),
            P(HEAD),
            P(HEAD, None),
        ),
        out_specs=P((TM, HEAD), None),
        check_vma=False,
    )
```
